512 devices in a mesh: gy: 32 (over x, y, core), gz: 16 (over z).
Axes of the slice: x: 4, y: 4, z: 16, core: 2. Of those that a mesh axis runs over, the one named last changes fastest.
Arguments:
- volume: bfloat16 [64, 128, 64, 256], P(None, 'gy', 'gz'), may hold values from -2500 to 2500
- down_weight: bfloat16 [128, 64, 2, 2, 2], replicated, may hold values from -0.25 to 0.25
- conv_one: bfloat16 [3, 3, 128, 384], replicated, may hold values from -0.109375 to 0.109375
- conv_two: bfloat16 [3, 3, 128, 384], replicated, may hold values from -0.109375 to 0.109375
- norm_gain: float32 [3, 128], replicated, may hold values from 0.1 to 1.9
- norm_shift: float32 [3, 128], replicated, may hold values from -2.5 to 2.5
Outputs:
- features: bfloat16 [128, 64, 32, 128], P(None, 'gy', 'gz')
The draws below stay inside these ranges and needn't reach their ends.
All inputs are finite; a program needn't handle non-finite values.
Results may differ from the reference program's by a relative error of at most 0.0065.
Values may be sent and summed in bfloat16 or wider, within the bound.
No kernel may reach another device: no remote copies, remote signals or barrier semaphores. Data moves between devices by JAX's collectives and lax.ppermute only.
A program may use at most 64 MiB of HBM per device.

```python
import math
from functools import partial
import jax
import jax.numpy as jnp
from jax import lax

CI = 64
CO = 128
YD = 2
YQ = 128
ZQ = 64
XQ = 256
N_GY = 32


def draw_volume(key, part):
    key_noise = jax.random.fold_in(key, 11)
    key_scale = jax.random.fold_in(key, 12)
    key_region = jax.random.fold_in(key, 13)
    key_offset = jax.random.fold_in(key, 14)
    key_channel = jax.random.fold_in(key, 15)
    key_base = jax.random.fold_in(key, 16)
    row_ramp = jnp.arange(YQ, dtype=jnp.float32) / (YQ - 1)
    depth_ramp = jnp.arange(ZQ, dtype=jnp.float32) / (ZQ - 1)
    row_region = jnp.arange(YQ, dtype=jnp.int32) * 4 // YQ
    depth_region = jnp.arange(ZQ, dtype=jnp.int32) * 4 // ZQ
    rough = jnp.exp(jax.random.uniform(key_scale, (YQ, ZQ, XQ), jnp.float32, 0.0, math.log(3.0)))
    region_gain = jnp.exp(jax.random.uniform(key_region, (4, 4), jnp.float32, 0.0, math.log(3.0)))
    region_field = region_gain[row_region][:, depth_region]
    offsets = jax.random.uniform(key_offset, (CI, 4, 4), jnp.float32, -2.0, 2.0)
    offset_field = offsets[:, row_region][:, :, depth_region]
    channel = jnp.exp(jax.random.uniform(key_channel, (CI,), jnp.float32, -0.4, 0.4))
    log_base = jax.random.uniform(key_base, (), jnp.float32, math.log(2.0), math.log(3.0))
    noise = jnp.clip(jax.random.normal(key_noise, (CI, YQ, ZQ, XQ), jnp.float32), -4.0, 4.0)
    ramp = jnp.exp(log_base * (row_ramp[:, None] + depth_ramp[None, :]))
    spatial = rough * (region_field * ramp)[:, :, None]
    values = (noise + offset_field[:, :, :, None]) * spatial[None] * channel[:, None, None, None]
    return values.astype(jnp.bfloat16)


def normal_values(key, shape, scale, reach, kind=jnp.bfloat16):
    array = scale * jax.random.normal(key, shape, jnp.float32)
    return jnp.clip(array, min=-reach, max=reach).astype(kind)


def setup_inputs(seed: int = 0) -> dict:
    seeds = jax.random.split(jax.random.key(seed), 7)
    return {
        "volume": draw_volume(jax.random.fold_in(seeds[6], 71), 0),
        "down_weight": normal_values(seeds[1], (CO, CI, 2, 2, 2), (CI * 8) ** -0.5, 0.25),
        "conv_one": normal_values(seeds[2], (3, 3, CO, 3 * CO), (27 * CO) ** -0.5, 0.109375),
        "conv_two": normal_values(seeds[3], (3, 3, CO, 3 * CO), (27 * CO) ** -0.5, 0.109375),
        "norm_gain": jnp.clip(1.0 + 0.18 * jax.random.normal(seeds[4], (3, CO), jnp.float32), 0.1, 1.9),
        "norm_shift": normal_values(seeds[5], (3, CO), 0.5, 2.5, jnp.float32),
    }


def leaky(value):
    return jnp.where(value >= 0.0, value, 0.01 * value)

def normalize(value, gain, shift):
    mean = lax.optimization_barrier(jnp.mean(value, axis=(1, 2, 3), keepdims=True))
    spread = lax.optimization_barrier(jnp.mean(jnp.square(value - mean), axis=(1, 2, 3), keepdims=True))
    scaled = (value - mean) / jnp.sqrt(spread + 1e-05)
    return leaky(scaled * gain[:, None, None, None] + shift[:, None, None, None])

def strided_block(volume, down_weight, index):
    start = (index * (2 * YD)).astype(jnp.int32)
    rows_in = lax.dynamic_slice_in_dim(volume, start, 2 * YD, 1).astype(jnp.float32)
    blocks = rows_in.reshape(CI, YD, 2, ZQ // 2, 2, XQ // 2, 2)
    return jnp.einsum('oiabc,iyazbxc->oyzx', down_weight.astype(jnp.float32), blocks, precision=lax.Precision.HIGHEST)

def convolve(field, conv_weight):
    kernel = conv_weight.astype(jnp.float32).reshape(3, 3, CO, 3, CO)
    kernel = jnp.transpose(kernel, (2, 4, 0, 1, 3))
    result = lax.conv_general_dilated(field.astype(jnp.float32)[None], kernel, (1, 1, 1), ((1, 1), (1, 1), (1, 1)), dimension_numbers=('NCDHW', 'OIDHW', 'NCDHW'), precision=lax.Precision.HIGHEST)
    return result[0]

def reference(volume, down_weight, conv_one, conv_two, norm_gain, norm_shift):
    coarse = lax.map(partial(strided_block, volume, down_weight), jnp.arange(N_GY, dtype=jnp.int32))
    coarse = jnp.moveaxis(coarse, 0, 1).reshape(CO, YD * N_GY, ZQ // 2, XQ // 2)
    first = normalize(coarse, norm_gain[0], norm_shift[0]).astype(jnp.bfloat16)
    second = normalize(convolve(first, conv_one), norm_gain[1], norm_shift[1]).astype(jnp.bfloat16)
    return normalize(convolve(second, conv_two), norm_gain[2], norm_shift[2]).astype(jnp.bfloat16)
```

```python
import jax
import jax.numpy as jnp
from jax import lax
from jax.sharding import Mesh
from jax.sharding import PartitionSpec as P

ROWS = ("x", "y", "core")
DEPTH = "z"


def rim(value, axis, dim):
    count, length = (lax.axis_size(axis), value.shape[dim])
    up = [(i, i + 1) for i in range(count - 1)]
    down = [(j, i) for i, j in up]
    before = lax.ppermute(lax.slice_in_dim(value, length - 1, length, axis=dim), axis, up)
    after = lax.ppermute(lax.slice_in_dim(value, 0, 1, axis=dim), axis, down)
    return before, after


def merged(stats, axis, count):
    parts = lax.axis_size(axis)
    sent = jnp.broadcast_to(stats[None], (parts,) + stats.shape)
    held = lax.all_to_all(sent, axis, 0, 0)
    mean = jnp.mean(held[:, 0], axis=0)
    apart = held[:, 0] - mean
    spread = jnp.sum(held[:, 1] + count * (apart * apart), axis=0)
    return jnp.stack([mean, spread])


def local_moments(inner):
    mean = jnp.mean(inner, axis=(1, 2, 3))
    centered = inner - mean[:, None, None, None]
    return jnp.stack([mean, jnp.sum(centered * centered, axis=(1, 2, 3))])


def moments(inner, with_rim):
    count = float(inner.shape[1] * inner.shape[2] * inner.shape[3])
    stats = local_moments(inner)
    wide = inner
    if with_rim:
        before, after = rim(wide, DEPTH, 2)
    stats = merged(stats, ROWS, count)
    count *= lax.axis_size(ROWS)
    if with_rim:
        wide = jnp.concatenate([before, wide, after], axis=2)
        before, after = rim(wide, ROWS, 1)
    stats = merged(stats, DEPTH, count)
    count *= lax.axis_size(DEPTH)
    if with_rim:
        wide = jnp.concatenate([before, wide, after], axis=1)
    return stats[0], stats[1] / count, wide


def leaky(value):
    return jnp.where(value >= 0.0, value, 0.01 * value)


def normalize(value, mean, spread, gain, shift):
    scaled = (value - mean[:, None, None, None]) / jnp.sqrt(spread + 1e-05)[:, None, None, None]
    return leaky(scaled * gain[:, None, None, None] + shift[:, None, None, None]).astype(jnp.bfloat16)


def inside(axis, length):
    index, count = lax.axis_index(axis), lax.axis_size(axis)
    plane = jnp.arange(length)
    first = (plane > 0) | (index > 0)
    last = (plane < length - 1) | (index < count - 1)
    return first & last


def padded(wide, mean, spread, gain, shift):
    value = normalize(wide, mean, spread, gain, shift)
    keep = inside(ROWS, wide.shape[1])[:, None] & inside(DEPTH, wide.shape[2])[None, :]
    return jnp.where(keep[None, :, :, None], value, jnp.zeros_like(value))


def strided(volume, down_weight):
    blocks = volume.reshape(
        volume.shape[0], volume.shape[1] // 2, 2, volume.shape[2] // 2, 2, volume.shape[3] // 2, 2
    )
    return jnp.einsum(
        "oiabc,iyazbxc->oyzx", down_weight, blocks, preferred_element_type=jnp.float32
    )


def convolve(field, conv_weight):
    rows, depth, length = (field.shape[1] - 2, field.shape[2] - 2, field.shape[3])
    widened = jnp.pad(field, ((0, 0), (0, 0), (0, 0), (1, 1)))
    stacked = jnp.concatenate(
        [widened[:, :, :, offset : offset + length] for offset in range(3)], axis=0
    )
    total = jnp.zeros((conv_weight.shape[2], rows, depth, length), jnp.float32)
    for row_tap in range(3):
        for depth_tap in range(3):
            piece = stacked[:, row_tap : row_tap + rows, depth_tap : depth_tap + depth, :]
            total = total + jnp.einsum(
                "ok,kyzx->oyzx",
                conv_weight[row_tap, depth_tap],
                piece,
                preferred_element_type=jnp.float32,
            )
    return total


def on_device(volume, down_weight, conv_one, conv_two, norm_gain, norm_shift):
    coarse = strided(volume, down_weight)
    mean, spread, wide = moments(coarse, True)
    first = padded(wide, mean, spread, norm_gain[0], norm_shift[0])
    middle = convolve(first, conv_one)
    mean, spread, wide = moments(middle, True)
    second = padded(wide, mean, spread, norm_gain[1], norm_shift[1])
    last = convolve(second, conv_two)
    mean, spread, _ = moments(last, False)
    return normalize(last, mean, spread, norm_gain[2], norm_shift[2])


def solution(mesh):
    split = Mesh(mesh.devices.reshape(4, 4, 2, 16), ROWS + (DEPTH,))
    return jax.shard_map(
        on_device,
        mesh=split,
        in_specs=(P(None, ROWS, DEPTH, None), P(), P(), P(), P(), P()),
        out_specs=P(None, ROWS, DEPTH, None),
        check_vma=False,
    )
```

```python
import functools

import jax
import jax.numpy as jnp
from jax import lax
from jax.experimental import pallas as pl
from jax.experimental.pallas import tpu as pltpu
from jax.sharding import Mesh
from jax.sharding import PartitionSpec as P


ROWS = ("x", "y", "core")
DEPTH = "z"


def neighbours(value, axis):
    count = lax.axis_size(axis)
    up = [(i, i + 1) for i in range(count - 1)]
    down = [(j, i) for i, j in up]
    before = lax.ppermute(value, axis, up)
    after = lax.ppermute(value, axis, down)
    return before, after


def pooled(stats, axis, count):
    parts = lax.axis_size(axis)
    sent = jnp.broadcast_to(stats[None], (parts,) + stats.shape)
    held = lax.all_to_all(sent, axis, 0, 0)
    mean = jnp.mean(held[:, 0], axis=0)
    apart = held[:, 0] - mean
    spread = jnp.sum(held[:, 1] + count * (apart * apart), axis=0)
    return jnp.stack([mean, spread])


def affine(stats, count, gain, shift):
    scale = gain / jnp.sqrt(stats[1] / count + 1e-05)
    return jnp.stack([stats[0], scale, shift])


def inside(axis, own, rim):
    plane = lax.axis_index(axis) * own - rim + jnp.arange(own + 2 * rim)
    return ((plane >= 0) & (plane < own * lax.axis_size(axis))).astype(jnp.float32)


def leaky(value):
    return jnp.where(value >= 0.0, value, 0.01 * value)


def conv_kernel(pieces, rows, depth, rim, keep, norm, *refs):
    fields, (source, out, stats, stacked, weight, arrived) = refs[:pieces], refs[pieces:]
    fetches = [
        pltpu.make_async_copy(source.at[tap], weight.at[tap], arrived.at[tap]) for tap in range(3)
    ]
    for fetch in fetches:
        fetch.start()
    length, channels = fields[0].shape[2:]
    each = rows // pieces
    mean, scale, shift = norm[0:1, :], norm[1:2, :], norm[2:3, :]
    place = lax.broadcasted_iota(jnp.int32, (length, channels), 0)

    for piece, field in enumerate(fields):
        @pl.loop(0, each * depth)
        def _(index, piece=piece, field=field):
            row, cell = index // depth, index % depth
            value = (field[row, cell] - mean) * scale + shift
            value = leaky(value) * keep[piece * each * depth + index]
            left = jnp.where(place > 0, pltpu.roll(value, 1, 0), 0.0)
            right = jnp.where(place < length - 1, pltpu.roll(value, length - 1, 0), 0.0)
            at = piece * each * depth + index
            stacked[at, :, 0:channels] = left.astype(jnp.bfloat16)
            stacked[at, :, channels : 2 * channels] = value.astype(jnp.bfloat16)
            stacked[at, :, 2 * channels :] = right.astype(jnp.bfloat16)

    cells = depth - 2
    for fetch in fetches:
        fetch.wait()

    def row_of(row):
        total = jnp.zeros((cells * length, channels), jnp.float32)
        for row_tap in range(3):
            for depth_tap in range(3):
                start = (row + row_tap) * depth + depth_tap
                piece = stacked[pl.ds(start, cells)].reshape(cells * length, 3 * channels)
                total = total + lax.dot_general(
                    piece,
                    weight[row_tap, depth_tap],
                    (((1,), (1,)), ((), ())),
                    preferred_element_type=jnp.float32,
                )
        out[row] = total.reshape(cells, length, channels)

    for row in range(rows - 2):
        row_of(row)

    inner = [
        out[row, cell]
        for row in range(rim, rows - 2 - rim)
        for cell in range(rim, cells - rim)
    ]
    middle = sum(jnp.sum(plane, axis=0, keepdims=True) for plane in inner) / (len(inner) * length)
    apart = [plane - middle for plane in inner]
    spread = sum(jnp.sum(plane * plane, axis=0, keepdims=True) for plane in apart)
    stats[0:1, :] = middle
    stats[1:2, :] = spread


def convolve(fields, weight, keep, norm, rim):
    pieces = len(fields)
    rows = pieces * fields[0].shape[0]
    depth, length, channels = fields[0].shape[1:]
    in_vmem = pl.BlockSpec(memory_space=pltpu.VMEM)
    flops = 2 * (rows - 2) * (depth - 2) * length * channels * channels * 27
    return pl.pallas_call(
        functools.partial(conv_kernel, pieces, rows, depth, rim),
        out_shape=(
            jax.ShapeDtypeStruct((rows - 2, depth - 2, length, channels), jnp.float32),
            jax.ShapeDtypeStruct((2, channels), jnp.float32),
        ),
        in_specs=[pl.BlockSpec(memory_space=pltpu.SMEM), in_vmem] + [in_vmem] * pieces
        + [pl.BlockSpec(memory_space=pltpu.HBM)],
        out_specs=(in_vmem, in_vmem),
        scratch_shapes=[
            pltpu.VMEM((rows * depth, length, 3 * channels), jnp.bfloat16),
            pltpu.VMEM(weight.shape, weight.dtype),
            pltpu.SemaphoreType.DMA((3,)),
        ],
        compiler_params=pltpu.CompilerParams(vmem_limit_bytes=16 << 20),
        cost_estimate=pl.CostEstimate(flops=flops, bytes_accessed=2 << 20, transcendentals=0),
    )(keep.reshape(-1), norm, *fields, pltpu.with_memory_space_constraint(weight, pltpu.HBM))


def strided(volume, down_weight):
    blocks = volume.reshape(
        volume.shape[0], volume.shape[1] // 2, 2, volume.shape[2] // 2, 2, volume.shape[3] // 2, 2
    )
    return jnp.einsum(
        "oiabc,iyazbxc->yzxo", down_weight, blocks, preferred_element_type=jnp.float32
    )


def local_moments(inner):
    mean = jnp.mean(inner, axis=(0, 1, 2))
    centered = inner - mean
    return jnp.stack([mean, jnp.sum(centered * centered, axis=(0, 1, 2))])


def on_device(volume, down_weight, conv_one, conv_two, norm_gain, norm_shift):
    coarse = strided(volume, down_weight)
    rows, depth, length = coarse.shape[:3]
    own = float(rows * depth * length)
    plane = own * lax.axis_size(ROWS)
    count = plane * lax.axis_size(DEPTH)
    wide_keep = inside(ROWS, rows, 2)[:, None] * inside(DEPTH, depth, 2)[None, :]
    keep = wide_keep[1:-1, 1:-1]

    before, after = neighbours(coarse, DEPTH)
    stats = pooled(local_moments(coarse), ROWS, own)
    wide = jnp.concatenate([before, coarse, after], axis=1)
    before, after = neighbours(wide, ROWS)
    stats = pooled(stats, DEPTH, plane)
    norm = affine(stats, count, norm_gain[0], norm_shift[0])
    middle, stats = convolve([before, wide, after], conv_one, wide_keep, norm, 1)
    stats = pooled(pooled(stats, ROWS, own), DEPTH, plane)
    norm = affine(stats, count, norm_gain[1], norm_shift[1])
    last, stats = convolve([middle], conv_two, keep, norm, 0)
    stats = pooled(pooled(stats, ROWS, own), DEPTH, plane)
    mean, scale, shift = affine(stats, count, norm_gain[2], norm_shift[2])
    features = leaky((last - mean) * scale + shift).astype(jnp.bfloat16)
    return jnp.transpose(features, (3, 0, 1, 2))


def solution(mesh):
    split = Mesh(mesh.devices.reshape(4, 4, 2, 16), ROWS + (DEPTH,))
    return jax.shard_map(
        on_device,
        mesh=split,
        in_specs=(P(None, ROWS, DEPTH, None), P(), P(), P(), P(), P()),
        out_specs=P(None, ROWS, DEPTH, None),
        check_vma=False,
    )
```

```python
import functools

import jax
import jax.numpy as jnp
from jax import lax
from jax.experimental import pallas as pl
from jax.experimental.pallas import tpu as pltpu
from jax.sharding import Mesh
from jax.sharding import PartitionSpec as P


ROWS = ("x", "y", "core")
DEPTH = "z"


def swaps(value, axis):
    count = lax.axis_size(axis)
    even = [(i, i + 1) for i in range(0, count - 1, 2)]
    odd = [(i, i + 1) for i in range(1, count - 1, 2)]
    got = []
    for pairs in (even, odd):
        got.append(lax.ppermute(value, axis, pairs + [(j, i) for i, j in pairs]))
    return got


def exchanged(stats, axis):
    sent = jnp.broadcast_to(stats[None], (lax.axis_size(axis),) + stats.shape)
    return lax.all_to_all(sent, axis, 0, 0)


def pooled(held, count):
    mean = jnp.mean(held[:, 0], axis=0)
    apart = held[:, 0] - mean
    spread = jnp.sum(held[:, 1] + count * (apart * apart), axis=0)
    return jnp.stack([mean, spread])


def affine(held, count, gain, shift):
    parts = held.shape[0]
    means = [held[part, 0:1, :] for part in range(parts)]
    mean = sum(means) / parts
    spread = sum(
        held[part, 1:2, :] + count * ((means[part] - mean) * (means[part] - mean))
        for part in range(parts)
    )
    return mean, gain / jnp.sqrt(spread / (count * parts) + 1e-05), shift


def leaky(value):
    return jnp.where(value >= 0.0, value, 0.01 * value)


def orders(at, own, swapped):
    if not swapped:
        return [(0, 0, own)]
    odd = lax.rem(at, 2)
    return [(0, own, own), (own, (1 - odd) * 2 * own, own), (2 * own, odd * 2 * own, own)]


def conv_kernel(norm, count, block, whole, rim, swapped, at, held, gains, *refs):
    pieces = 3 if swapped else 1
    fields, (source, out, stats, stacked, weight, arrived) = refs[:pieces], refs[pieces:]
    length, channels = fields[0].shape[2:]
    rows, depth = pieces * fields[0].shape[0], fields[0].shape[1]
    wide = 3 * channels
    fetches = [
        pltpu.make_async_copy(
            source.at[row_tap, depth_tap],
            weight.at[pl.ds(row_tap * channels, channels), pl.ds(depth_tap * wide, wide)],
            arrived.at[row_tap, depth_tap],
        )
        for row_tap in range(3)
        for depth_tap in range(3)
    ]
    for fetch in fetches:
        fetch.start()

    mean, scale, shift = affine(held, count, gains[0, norm : norm + 1, :], gains[1, norm : norm + 1, :])
    place = lax.broadcasted_iota(jnp.int32, (length, channels), 0)
    row_at = at[0] * block[0] - (rows - block[0]) // 2
    depth_at = at[1] * block[1] - (depth - block[1]) // 2
    row_groups = orders(at[0], block[0] if swapped else rows, swapped)
    depth_groups = orders(at[1], block[1] if swapped else depth, swapped)
    for piece, (_, to_row, row_count) in enumerate(row_groups):
        for from_cell, to_cell, cell_count in depth_groups:
            for i in range(row_count):
                for j in range(cell_count):
                    row, cell = to_row + i, to_cell + j
                    y, z = row_at + row, depth_at + cell
                    here = (y >= 0) & (y < whole[0]) & (z >= 0) & (z < whole[1])
                    value = (fields[piece][i, from_cell + j] - mean) * scale + shift
                    value = jnp.maximum(value, 0.01 * value) * jnp.where(here, 1.0, 0.0)
                    left = jnp.where(place > 0, pltpu.roll(value, 1, 0), 0.0)
                    right = jnp.where(place < length - 1, pltpu.roll(value, length - 1, 0), 0.0)
                    slot = row * depth + cell
                    stacked[slot, :, 0:channels] = left.astype(jnp.bfloat16)
                    stacked[slot, :, channels : 2 * channels] = value.astype(jnp.bfloat16)
                    stacked[slot, :, 2 * channels :] = right.astype(jnp.bfloat16)

    for fetch in fetches:
        fetch.wait()

    cells = depth - 2
    for row in range(rows):
        taken = jnp.concatenate(
            [
                stacked[pl.ds(row * depth + depth_tap, cells)].reshape(cells * length, wide)
                for depth_tap in range(3)
            ],
            axis=1,
        )
        taps = [tap for tap in range(3) if 0 <= row - tap < rows - 2]
        product = lax.dot_general(
            taken,
            weight[pl.ds(taps[0] * channels, len(taps) * channels), :],
            (((1,), (1,)), ((), ())),
            preferred_element_type=jnp.float32,
        )
        for place_of, tap in enumerate(taps):
            part = product[:, place_of * channels : (place_of + 1) * channels]
            part = part.reshape(cells, length, channels)
            if tap == 0:
                out[row] = part
            else:
                out[row - tap] += part

    inner = [
        out[row, cell]
        for row in range(rim, rows - 2 - rim)
        for cell in range(rim, cells - rim)
    ]
    middle = sum(jnp.sum(plane, axis=0, keepdims=True) for plane in inner) / (len(inner) * length)
    apart = [plane - middle for plane in inner]
    spread = sum(jnp.sum(plane * plane, axis=0, keepdims=True) for plane in apart)
    stats[0:1, :] = middle
    stats[1:2, :] = spread


def convolve(norm, count, block, whole, rim, at, held, gains, fields, weight):
    pieces = len(fields)
    rows = pieces * fields[0].shape[0]
    depth, length, channels = fields[0].shape[1:]
    in_vmem = pl.BlockSpec(memory_space=pltpu.VMEM)
    flops = 2 * (rows - 2) * (depth - 2) * length * channels * channels * 27
    return pl.pallas_call(
        functools.partial(conv_kernel, norm, count, block, whole, rim, pieces == 3),
        out_shape=(
            jax.ShapeDtypeStruct((rows - 2, depth - 2, length, channels), jnp.float32),
            jax.ShapeDtypeStruct((2, channels), jnp.float32),
        ),
        in_specs=[pl.BlockSpec(memory_space=pltpu.SMEM)]
        + [in_vmem] * (2 + pieces)
        + [pl.BlockSpec(memory_space=pltpu.HBM)],
        out_specs=(in_vmem, in_vmem),
        scratch_shapes=[
            pltpu.VMEM((rows * depth, length, 3 * channels), jnp.bfloat16),
            pltpu.VMEM((3 * channels, 9 * channels), weight.dtype),
            pltpu.SemaphoreType.DMA((3, 3)),
        ],
        compiler_params=pltpu.CompilerParams(vmem_limit_bytes=16 << 20),
        cost_estimate=pl.CostEstimate(flops=flops, bytes_accessed=2 << 20, transcendentals=0),
    )(at, held, gains, *fields, pltpu.with_memory_space_constraint(weight, pltpu.HBM))


def strided(volume, down_weight):
    blocks = volume.reshape(
        volume.shape[0], volume.shape[1] // 2, 2, volume.shape[2] // 2, 2, volume.shape[3] // 2, 2
    )
    return jnp.einsum(
        "oiabc,iyazbxc->yzxo", down_weight, blocks, preferred_element_type=jnp.float32
    )


def local_moments(inner):
    mean = jnp.mean(inner, axis=(0, 1, 2))
    centered = inner - mean
    return jnp.stack([mean, jnp.sum(centered * centered, axis=(0, 1, 2))])


def on_device(volume, down_weight, conv_one, conv_two, norm_gain, norm_shift):
    coarse = strided(volume, down_weight)
    rows, depth, length = coarse.shape[:3]
    block = (rows, depth)
    whole = (rows * lax.axis_size(ROWS), depth * lax.axis_size(DEPTH))
    own = float(rows * depth * length)
    plane = own * lax.axis_size(ROWS)
    at = jnp.stack([lax.axis_index(ROWS), lax.axis_index(DEPTH)])
    gains = jnp.stack([norm_gain, norm_shift])

    stats, at, gains, gain, shift = lax.optimization_barrier(
        (local_moments(coarse), at, gains, norm_gain[2], norm_shift[2])
    )
    beside = swaps(coarse, DEPTH)
    stats = pooled(exchanged(stats, ROWS), own)
    wide = jnp.concatenate([coarse] + beside, axis=1)
    beside = swaps(wide, ROWS)
    held = exchanged(stats, DEPTH)
    middle, stats = convolve(0, plane, block, whole, 1, at, held, gains, [wide] + beside, conv_one)
    held = exchanged(pooled(exchanged(stats, ROWS), own), DEPTH)
    last, stats = convolve(1, plane, block, whole, 0, at, held, gains, [middle], conv_two)
    held = exchanged(pooled(exchanged(stats, ROWS), own), DEPTH)
    mean, spread = pooled(held, plane)
    scale = gain / jnp.sqrt(spread / (plane * held.shape[0]) + 1e-05)
    features = leaky((last - mean) * scale + shift).astype(jnp.bfloat16)
    return jnp.transpose(features, (3, 0, 1, 2))


def solution(mesh):
    split = Mesh(mesh.devices.reshape(4, 4, 2, 16), ROWS + (DEPTH,))
    return jax.shard_map(
        on_device,
        mesh=split,
        in_specs=(P(None, ROWS, DEPTH, None), P(), P(), P(), P(), P()),
        out_specs=P(None, ROWS, DEPTH, None),
        check_vma=False,
    )
```

```python
import functools

import jax
import jax.numpy as jnp
from jax import lax
from jax.experimental import pallas as pl
from jax.experimental.pallas import tpu as pltpu
from jax.sharding import Mesh
from jax.sharding import PartitionSpec as P


ROWS = ("x", "y", "core")
DEPTH = "z"


def swaps(value, axis):
    count = lax.axis_size(axis)
    even = [(i, i + 1) for i in range(0, count - 1, 2)]
    odd = [(i, i + 1) for i in range(1, count - 1, 2)]
    got = []
    for pairs in (even, odd):
        got.append(lax.ppermute(value, axis, pairs + [(j, i) for i, j in pairs]))
    return got


def exchanged(stats, axis):
    sent = jnp.broadcast_to(stats[None], (lax.axis_size(axis),) + stats.shape)
    return lax.all_to_all(sent, axis, 0, 0)


def pooled(held, count):
    mean = jnp.mean(held[:, 0], axis=0)
    apart = held[:, 0] - mean
    spread = jnp.sum(held[:, 1] + count * (apart * apart), axis=0)
    return jnp.stack([mean, spread])


def affine(held, count, gain, shift):
    parts = held.shape[0]
    means = [held[part, 0:1, :] for part in range(parts)]
    mean = sum(means) / parts
    spread = sum(
        held[part, 1:2, :] + count * ((means[part] - mean) * (means[part] - mean))
        for part in range(parts)
    )
    return mean, gain / jnp.sqrt(spread / (count * parts) + 1e-05), shift


def leaky(value):
    return jnp.where(value >= 0.0, value, 0.01 * value)


def orders(at, own, swapped):
    if not swapped:
        return [(0, 0, own)]
    odd = lax.rem(at, 2)
    return [(0, own, own), (own, (1 - odd) * 2 * own, own), (2 * own, odd * 2 * own, own)]


def conv_kernel(norm, count, block, whole, rim, swapped, at, held, gains, *refs):
    pieces = 3 if swapped else 1
    fields, (source, out, stats, stacked, weight, arrived) = refs[:pieces], refs[pieces:]
    length, channels = fields[0].shape[2:]
    rows, depth = pieces * fields[0].shape[0], fields[0].shape[1]
    wide = 3 * channels
    fetches = [
        pltpu.make_async_copy(
            source.at[row_tap, depth_tap],
            weight.at[pl.ds(row_tap * channels, channels), pl.ds(depth_tap * wide, wide)],
            arrived.at[row_tap, depth_tap],
        )
        for row_tap in range(3)
        for depth_tap in range(3)
    ]
    for fetch in fetches:
        fetch.start()

    mean, scale, shift = affine(held, count, gains[0, norm : norm + 1, :], gains[1, norm : norm + 1, :])
    place = lax.broadcasted_iota(jnp.int32, (length, channels), 0)
    row_at = at[0] * block[0] - (rows - block[0]) // 2
    depth_at = at[1] * block[1] - (depth - block[1]) // 2
    row_groups = orders(at[0], block[0] if swapped else rows, swapped)
    depth_groups = orders(at[1], block[1] if swapped else depth, swapped)
    for piece, (_, to_row, row_count) in enumerate(row_groups):
        for from_cell, to_cell, cell_count in depth_groups:
            for i in range(row_count):
                for j in range(cell_count):
                    row, cell = to_row + i, to_cell + j
                    y, z = row_at + row, depth_at + cell
                    here = (y >= 0) & (y < whole[0]) & (z >= 0) & (z < whole[1])
                    value = (fields[piece][i, from_cell + j] - mean) * scale + shift
                    value = jnp.maximum(value, 0.01 * value) * jnp.where(here, 1.0, 0.0)
                    left = jnp.where(place > 0, pltpu.roll(value, 1, 0), 0.0)
                    right = jnp.where(place < length - 1, pltpu.roll(value, length - 1, 0), 0.0)
                    slot = row * depth + cell
                    stacked[slot, :, 0:channels] = left.astype(jnp.bfloat16)
                    stacked[slot, :, channels : 2 * channels] = value.astype(jnp.bfloat16)
                    stacked[slot, :, 2 * channels :] = right.astype(jnp.bfloat16)

    for fetch in fetches:
        fetch.wait()

    cells = depth - 2
    for row in range(rows):
        taken = jnp.concatenate(
            [
                stacked[pl.ds(row * depth + depth_tap, cells)].reshape(cells * length, wide)
                for depth_tap in range(3)
            ],
            axis=1,
        )
        taps = [tap for tap in range(3) if 0 <= row - tap < rows - 2]
        product = lax.dot_general(
            taken,
            weight[pl.ds(taps[0] * channels, len(taps) * channels), :],
            (((1,), (1,)), ((), ())),
            preferred_element_type=jnp.float32,
        )
        for place_of, tap in enumerate(taps):
            part = product[:, place_of * channels : (place_of + 1) * channels]
            part = part.reshape(cells, length, channels)
            if tap == 0:
                out[row] = part
            else:
                out[row - tap] += part

    inner = [
        out[row, cell]
        for row in range(rim, rows - 2 - rim)
        for cell in range(rim, cells - rim)
    ]
    middle = sum(jnp.sum(plane, axis=0, keepdims=True) for plane in inner) / (len(inner) * length)
    apart = [plane - middle for plane in inner]
    spread = sum(jnp.sum(plane * plane, axis=0, keepdims=True) for plane in apart)
    stats[0:1, :] = middle
    stats[1:2, :] = spread


def convolve(norm, count, block, whole, rim, at, held, gains, fields, weight):
    pieces = len(fields)
    rows = pieces * fields[0].shape[0]
    depth, length, channels = fields[0].shape[1:]
    in_vmem = pl.BlockSpec(memory_space=pltpu.VMEM)
    flops = 2 * (rows - 2) * (depth - 2) * length * channels * channels * 27
    return pl.pallas_call(
        functools.partial(conv_kernel, norm, count, block, whole, rim, pieces == 3),
        out_shape=(
            jax.ShapeDtypeStruct((rows - 2, depth - 2, length, channels), jnp.float32),
            jax.ShapeDtypeStruct((2, channels), jnp.float32),
        ),
        in_specs=[pl.BlockSpec(memory_space=pltpu.SMEM)]
        + [in_vmem] * (2 + pieces)
        + [pl.BlockSpec(memory_space=pltpu.HBM)],
        out_specs=(in_vmem, in_vmem),
        scratch_shapes=[
            pltpu.VMEM((rows * depth, length, 3 * channels), jnp.bfloat16),
            pltpu.VMEM((3 * channels, 9 * channels), weight.dtype),
            pltpu.SemaphoreType.DMA((3, 3)),
        ],
        compiler_params=pltpu.CompilerParams(vmem_limit_bytes=16 << 20),
        cost_estimate=pl.CostEstimate(flops=flops, bytes_accessed=2 << 20, transcendentals=0),
    )(at, held, gains, *fields, pltpu.with_memory_space_constraint(weight, pltpu.HBM))


def strided(volume, down_weight):
    blocks = volume.reshape(
        volume.shape[0], volume.shape[1] // 2, 2, volume.shape[2] // 2, 2, volume.shape[3] // 2, 2
    )
    return jnp.einsum(
        "oiabc,iyazbxc->yzxo", down_weight, blocks, preferred_element_type=jnp.float32
    )


def local_moments(inner):
    mean = jnp.mean(inner, axis=(0, 1, 2))
    centered = inner - mean
    return jnp.stack([mean, jnp.sum(centered * centered, axis=(0, 1, 2))])


def on_device(volume, down_weight, conv_one, conv_two, norm_gain, norm_shift):
    coarse = strided(volume, down_weight)
    rows, depth, length = coarse.shape[:3]
    block = (rows, depth)
    whole = (rows * lax.axis_size(ROWS), depth * lax.axis_size(DEPTH))
    own = float(rows * depth * length)
    plane = own * lax.axis_size(ROWS)
    at = jnp.stack([lax.axis_index(ROWS), lax.axis_index(DEPTH)])
    gains = jnp.stack([norm_gain, norm_shift])

    coarse, at, gains, gain, shift = lax.optimization_barrier(
        (coarse, at, gains, norm_gain[2], norm_shift[2])
    )

    stats = local_moments(coarse)
    beside = swaps(coarse, DEPTH)
    stats = pooled(exchanged(stats, ROWS), own)
    wide = jnp.concatenate([coarse] + beside, axis=1)
    beside = swaps(wide, ROWS)
    held = exchanged(stats, DEPTH)
    middle, stats = convolve(0, plane, block, whole, 1, at, held, gains, [wide] + beside, conv_one)
    held = exchanged(pooled(exchanged(stats, ROWS), own), DEPTH)
    last, stats = convolve(1, plane, block, whole, 0, at, held, gains, [middle], conv_two)
    held = exchanged(pooled(exchanged(stats, ROWS), own), DEPTH)
    mean, spread = pooled(held, plane)
    scale = gain / jnp.sqrt(spread / (plane * held.shape[0]) + 1e-05)
    features = leaky((last - mean) * scale + shift).astype(jnp.bfloat16)
    return jnp.transpose(features, (3, 0, 1, 2))


def solution(mesh):
    split = Mesh(mesh.devices.reshape(4, 4, 2, 16), ROWS + (DEPTH,))
    return jax.shard_map(
        on_device,
        mesh=split,
        in_specs=(P(None, ROWS, DEPTH, None), P(), P(), P(), P(), P()),
        out_specs=P(None, ROWS, DEPTH, None),
        check_vma=False,
    )
```

```python
import functools

import jax
import jax.numpy as jnp
from jax import lax
from jax.experimental import pallas as pl
from jax.experimental.pallas import tpu as pltpu
from jax.sharding import Mesh
from jax.sharding import PartitionSpec as P


ROWS = ("x", "y", "core")
DEPTH = "z"


def swaps(value, axis):
    count = lax.axis_size(axis)
    even = [(i, i + 1) for i in range(0, count - 1, 2)]
    odd = [(i, i + 1) for i in range(1, count - 1, 2)]
    got = []
    for pairs in (even, odd):
        got.append(lax.ppermute(value, axis, pairs + [(j, i) for i, j in pairs]))
    return got


def exchanged(stats, axis):
    sent = jnp.broadcast_to(stats[None], (lax.axis_size(axis),) + stats.shape)
    return lax.all_to_all(sent, axis, 0, 0)


def pooled(held, count):
    mean = jnp.mean(held[:, 0], axis=0)
    apart = held[:, 0] - mean
    spread = jnp.sum(held[:, 1] + count * (apart * apart), axis=0)
    return jnp.stack([mean, spread])


def affine(held, count, gain, shift):
    parts = held.shape[0]
    means = [held[part, 0:1, :] for part in range(parts)]
    mean = sum(means) / parts
    spread = sum(
        held[part, 1:2, :] + count * ((means[part] - mean) * (means[part] - mean))
        for part in range(parts)
    )
    return mean, gain / jnp.sqrt(spread / (count * parts) + 1e-05), shift


def leaky(value):
    return jnp.where(value >= 0.0, value, 0.01 * value)


def orders(at, own, swapped):
    if not swapped:
        return [(0, 0, own)]
    odd = lax.rem(at, 2)
    return [(0, own, own), (own, (1 - odd) * 2 * own, own), (2 * own, odd * 2 * own, own)]


def conv_kernel(norm, count, block, whole, rim, swapped, at, held, gains, shifts, *refs):
    pieces = 3 if swapped else 1
    fields, (source, out, stats, gain, moved, stacked, weight, arrived) = refs[:pieces], refs[pieces:]
    fetch = pltpu.make_async_copy(source, weight, arrived)
    fetch.start()
    length, channels = fields[0].shape[2:]
    rows, depth = len(fields) * fields[0].shape[0], fields[0].shape[1]

    mean, scale, shift = affine(held, count, gains[norm : norm + 1, :], shifts[norm : norm + 1, :])
    row_at = at[0] * block[0] - (rows - block[0]) // 2
    depth_at = at[1] * block[1] - (depth - block[1]) // 2
    row_groups = orders(at[0], block[0] if swapped else rows, swapped)
    depth_groups = orders(at[1], block[1] if swapped else depth, swapped)
    for piece, (_, to_row, row_count) in enumerate(row_groups):
        for from_cell, to_cell, cell_count in depth_groups:
            for i in range(row_count):
                for j in range(cell_count):
                    row, cell = to_row + i, to_cell + j
                    y, z = row_at + row, depth_at + cell
                    here = (y >= 0) & (y < whole[0]) & (z >= 0) & (z < whole[1])
                    keep = jnp.where(here, 1.0, 0.0)
                    value = (fields[piece][i, from_cell + j] - mean) * (scale * keep) + shift * keep
                    value = jnp.maximum(value, 0.01 * value)
                    stacked[row * depth + cell] = value.astype(jnp.bfloat16)

    fetch.wait()
    cells = depth - 2
    taps = jnp.concatenate(
        [
            jnp.concatenate(
                [weight[tap // 3, tap % 3, :, part * channels : (part + 1) * channels] for tap in range(9)],
                axis=1,
            )
            for part in range(3)
        ],
        axis=0,
    )
    place = lax.broadcasted_iota(jnp.int32, (length, channels), 0)
    for row in range(rows - 2):
        taken = jnp.concatenate(
            [
                stacked[pl.ds((row + tap // 3) * depth + tap % 3, cells)].reshape(cells * length, channels)
                for tap in range(9)
            ],
            axis=1,
        )
        product = lax.dot_general(
            taken, taps, (((1,), (1,)), ((), ())), preferred_element_type=jnp.float32
        )
        for cell in range(cells):
            before, here, after = (
                product[cell * length : (cell + 1) * length, part * channels : (part + 1) * channels]
                for part in range(3)
            )
            before = jnp.where(place > 0, pltpu.roll(before, 1, 0), 0.0)
            after = jnp.where(place < length - 1, pltpu.roll(after, length - 1, 0), 0.0)
            out[row, cell] = before + here + after

    inner = [
        out[row, cell]
        for row in range(rim, rows - 2 - rim)
        for cell in range(rim, cells - rim)
    ]
    middle = sum(jnp.sum(plane, axis=0, keepdims=True) for plane in inner) / (len(inner) * length)
    apart = [plane - middle for plane in inner]
    spread = sum(jnp.sum(plane * plane, axis=0, keepdims=True) for plane in apart)
    stats[0:1, :] = middle
    stats[1:2, :] = spread
    gain[...] = gains[norm + 1 : norm + 2, :]
    moved[...] = shifts[norm + 1 : norm + 2, :]


def convolve(norm, count, block, whole, rim, at, held, gains, shifts, fields, weight):
    pieces = len(fields)
    rows = pieces * fields[0].shape[0]
    depth, length, channels = fields[0].shape[1:]
    in_vmem = pl.BlockSpec(memory_space=pltpu.VMEM)
    flops = 2 * (rows - 2) * (depth - 2) * length * channels * channels * 27
    return pl.pallas_call(
        functools.partial(conv_kernel, norm, count, block, whole, rim, pieces == 3),
        out_shape=(
            jax.ShapeDtypeStruct((rows - 2, depth - 2, length, channels), jnp.float32),
            jax.ShapeDtypeStruct((2, channels), jnp.float32),
            jax.ShapeDtypeStruct((1, channels), jnp.float32),
            jax.ShapeDtypeStruct((1, channels), jnp.float32),
        ),
        in_specs=[pl.BlockSpec(memory_space=pltpu.SMEM)]
        + [in_vmem] * (3 + pieces)
        + [pl.BlockSpec(memory_space=pltpu.HBM)],
        out_specs=(in_vmem,) * 4,
        scratch_shapes=[
            pltpu.VMEM((rows * depth, length, channels), jnp.bfloat16),
            pltpu.VMEM(weight.shape, weight.dtype),
            pltpu.SemaphoreType.DMA(()),
        ],
        compiler_params=pltpu.CompilerParams(vmem_limit_bytes=16 << 20),
        cost_estimate=pl.CostEstimate(flops=flops, bytes_accessed=2 << 20, transcendentals=0),
    )(at, held, gains, shifts, *fields, pltpu.with_memory_space_constraint(weight, pltpu.HBM))


def strided(volume, down_weight):
    blocks = volume.reshape(
        volume.shape[0], volume.shape[1] // 2, 2, volume.shape[2] // 2, 2, volume.shape[3] // 2, 2
    )
    return jnp.einsum(
        "oiabc,iyazbxc->yzxo", down_weight, blocks, preferred_element_type=jnp.float32
    )


def local_moments(inner):
    mean = jnp.mean(inner, axis=(0, 1, 2))
    centered = inner - mean
    return jnp.stack([mean, jnp.sum(centered * centered, axis=(0, 1, 2))])


def on_device(volume, down_weight, conv_one, conv_two, norm_gain, norm_shift):
    coarse = strided(volume, down_weight)
    rows, depth, length = coarse.shape[:3]
    block = (rows, depth)
    whole = (rows * lax.axis_size(ROWS), depth * lax.axis_size(DEPTH))
    own = float(rows * depth * length)
    plane = own * lax.axis_size(ROWS)
    at = jnp.stack([lax.axis_index(ROWS), lax.axis_index(DEPTH)])
    coarse, at = lax.optimization_barrier((coarse, at))

    stats = local_moments(coarse)
    beside = swaps(coarse, DEPTH)
    stats = pooled(exchanged(stats, ROWS), own)
    wide = jnp.concatenate([coarse] + beside, axis=1)
    beside = swaps(wide, ROWS)
    held = exchanged(stats, DEPTH)
    middle, stats, _, _ = convolve(0, plane, block, whole, 1, at, held, norm_gain, norm_shift, [wide] + beside, conv_one)
    held = exchanged(pooled(exchanged(stats, ROWS), own), DEPTH)
    last, stats, gain, shift = convolve(1, plane, block, whole, 0, at, held, norm_gain, norm_shift, [middle], conv_two)
    held = exchanged(pooled(exchanged(stats, ROWS), own), DEPTH)
    mean, spread = pooled(held, plane)
    scale = gain[0] / jnp.sqrt(spread / (plane * held.shape[0]) + 1e-05)
    features = leaky((last - mean) * scale + shift[0]).astype(jnp.bfloat16)
    return jnp.transpose(features, (3, 0, 1, 2))


def solution(mesh):
    split = Mesh(mesh.devices.reshape(4, 4, 2, 16), ROWS + (DEPTH,))
    return jax.shard_map(
        on_device,
        mesh=split,
        in_specs=(P(None, ROWS, DEPTH, None), P(), P(), P(), P(), P()),
        out_specs=P(None, ROWS, DEPTH, None),
        check_vma=False,
    )
```

```python
import functools

import jax
import jax.numpy as jnp
from jax import lax
from jax.experimental import pallas as pl
from jax.experimental.pallas import tpu as pltpu
from jax.sharding import Mesh
from jax.sharding import PartitionSpec as P


ROWS = ("x", "y", "core")
DEPTH = "z"


def swaps(value, axis):
    count = lax.axis_size(axis)
    even = [(i, i + 1) for i in range(0, count - 1, 2)]
    odd = [(i, i + 1) for i in range(1, count - 1, 2)]
    got = []
    for pairs in (even, odd):
        got.append(lax.ppermute(value, axis, pairs + [(j, i) for i, j in pairs]))
    return got


def exchanged(stats, axis):
    sent = jnp.broadcast_to(stats[None], (lax.axis_size(axis),) + stats.shape)
    return lax.all_to_all(sent, axis, 0, 0)


def pooled(held, count):
    mean = jnp.mean(held[:, 0], axis=0)
    apart = held[:, 0] - mean
    spread = jnp.sum(held[:, 1] + count * (apart * apart), axis=0)
    return jnp.stack([mean, spread])


def affine(held, count, gain, shift):
    parts = held.shape[0]
    means = [held[part, 0:1, :] for part in range(parts)]
    mean = sum(means) / parts
    spread = sum(
        held[part, 1:2, :] + count * ((means[part] - mean) * (means[part] - mean))
        for part in range(parts)
    )
    return mean, gain / jnp.sqrt(spread / (count * parts) + 1e-05), shift


def leaky(value):
    return jnp.where(value >= 0.0, value, 0.01 * value)


def orders(at, own, swapped):
    if not swapped:
        return [(0, 0, own)]
    odd = lax.rem(at, 2)
    return [(0, own, own), (own, (1 - odd) * 2 * own, own), (2 * own, odd * 2 * own, own)]


def conv_kernel(norm, count, block, whole, rim, swapped, at, held, gains, shifts, *refs):
    pieces, results = (3, 2) if swapped else (2, 1)
    fields, weight, outs, (stats, gain, moved, stacked, *fetching) = (
        refs[:pieces],
        refs[pieces],
        refs[pieces + 1 : pieces + 1 + results],
        refs[pieces + 1 + results :],
    )
    if fetching:
        source, (weight, arrived) = weight, fetching
        fetch = pltpu.make_async_copy(source, weight, arrived)
        fetch.start()
    length, channels = fields[0].shape[2:]
    rows, depth = pieces * fields[0].shape[0], 3 * block[1] if swapped else block[1] + 2

    mean, scale, shift = affine(held, count, gains[norm : norm + 1, :], shifts[norm : norm + 1, :])
    row_at = at[0] * block[0] - (rows - block[0]) // 2
    depth_at = at[1] * block[1] - (depth - block[1]) // 2
    each = fields[0].shape[0]
    row_groups = orders(at[0], block[0], True) if swapped else [(i * each, i * each, each) for i in range(pieces)]
    depth_groups = orders(at[1], block[1] if swapped else depth, swapped)
    for piece, (_, to_row, row_count) in enumerate(row_groups):
        for from_cell, to_cell, cell_count in depth_groups:
            for i in range(row_count):
                for j in range(cell_count):
                    row, cell = to_row + i, to_cell + j
                    y, z = row_at + row, depth_at + cell
                    here = (y >= 0) & (y < whole[0]) & (z >= 0) & (z < whole[1])
                    keep = jnp.where(here, 1.0, 0.0)
                    value = (fields[piece][i, from_cell + j] - mean) * (scale * keep) + shift * keep
                    value = jnp.maximum(value, 0.01 * value)
                    stacked[row * depth + cell] = value.astype(jnp.bfloat16)

    if fetching:
        fetch.wait()
    cells = depth - 2
    out = {row: outs[row * results // (rows - 2)].at[row % ((rows - 2) // results)] for row in range(rows - 2)}
    taps = jnp.concatenate(
        [
            jnp.concatenate(
                [weight[tap // 3, tap % 3, :, part * channels : (part + 1) * channels] for tap in range(9)],
                axis=1,
            )
            for part in range(3)
        ],
        axis=0,
    )
    place = lax.broadcasted_iota(jnp.int32, (length, channels), 0)
    for row in range(rows - 2):
        taken = jnp.concatenate(
            [
                stacked[pl.ds((row + tap // 3) * depth + tap % 3, cells)].reshape(cells * length, channels)
                for tap in range(9)
            ],
            axis=1,
        )
        product = lax.dot_general(
            taken, taps, (((1,), (1,)), ((), ())), preferred_element_type=jnp.float32
        )
        for cell in range(cells):
            before, here, after = (
                product[cell * length : (cell + 1) * length, part * channels : (part + 1) * channels]
                for part in range(3)
            )
            before = jnp.where(place > 0, pltpu.roll(before, 1, 0), 0.0)
            after = jnp.where(place < length - 1, pltpu.roll(after, length - 1, 0), 0.0)
            out[row][cell] = before + here + after

    inner = [
        out[row][cell]
        for row in range(rim, rows - 2 - rim)
        for cell in range(rim, cells - rim)
    ]
    middle = sum(jnp.sum(plane, axis=0, keepdims=True) for plane in inner) / (len(inner) * length)
    apart = [plane - middle for plane in inner]
    spread = sum(jnp.sum(plane * plane, axis=0, keepdims=True) for plane in apart)
    stats[0:1, :] = middle
    stats[1:2, :] = spread
    gain[...] = gains[norm + 1 : norm + 2, :]
    moved[...] = shifts[norm + 1 : norm + 2, :]


def convolve(norm, count, block, whole, rim, at, held, gains, shifts, fields, weight):
    pieces = len(fields)
    swapped = pieces == 3
    each, wide, length, channels = fields[0].shape
    rows, depth = pieces * each, wide if swapped else block[1] + 2
    in_vmem = pl.BlockSpec(memory_space=pltpu.VMEM)
    flops = 2 * (rows - 2) * (depth - 2) * length * channels * channels * 27
    row = jax.ShapeDtypeStruct((1, channels), jnp.float32)
    out = jax.ShapeDtypeStruct((rows - 2, depth - 2, length, channels), jnp.float32)
    outs = [jax.ShapeDtypeStruct(fields[0].shape, jnp.float32)] * 2 if swapped else [out]
    outs += [jax.ShapeDtypeStruct((2, channels), jnp.float32), row, row]
    scratch = [pltpu.VMEM((rows * depth, length, channels), jnp.bfloat16)]
    if swapped:
        scratch += [pltpu.VMEM(weight.shape, weight.dtype), pltpu.SemaphoreType.DMA(())]
        weight = pltpu.with_memory_space_constraint(weight, pltpu.HBM)
    return pl.pallas_call(
        functools.partial(conv_kernel, norm, count, block, whole, rim, swapped),
        out_shape=outs,
        in_specs=[pl.BlockSpec(memory_space=pltpu.SMEM)] + [in_vmem] * (3 + pieces)
        + [pl.BlockSpec(memory_space=pltpu.HBM) if swapped else in_vmem],
        out_specs=[in_vmem] * len(outs),
        scratch_shapes=scratch,
        input_output_aliases={5: 0, 6: 1} if swapped else {},
        compiler_params=pltpu.CompilerParams(vmem_limit_bytes=16 << 20),
        cost_estimate=pl.CostEstimate(flops=flops, bytes_accessed=2 << 20, transcendentals=0),
    )(at, held, gains, shifts, *fields, weight)


def strided(volume, down_weight):
    blocks = volume.reshape(
        volume.shape[0], volume.shape[1] // 2, 2, volume.shape[2] // 2, 2, volume.shape[3] // 2, 2
    )
    return jnp.einsum(
        "oiabc,iyazbxc->yzxo", down_weight, blocks, preferred_element_type=jnp.float32
    )


def local_moments(inner):
    mean = jnp.mean(inner, axis=(0, 1, 2))
    centered = inner - mean
    return jnp.stack([mean, jnp.sum(centered * centered, axis=(0, 1, 2))])


def on_device(volume, down_weight, conv_one, conv_two, norm_gain, norm_shift):
    coarse = strided(volume, down_weight)
    rows, depth, length = coarse.shape[:3]
    block = (rows, depth)
    whole = (rows * lax.axis_size(ROWS), depth * lax.axis_size(DEPTH))
    own = float(rows * depth * length)
    plane = own * lax.axis_size(ROWS)
    at = jnp.stack([lax.axis_index(ROWS), lax.axis_index(DEPTH)])
    coarse, at = lax.optimization_barrier((coarse, at))

    stats = local_moments(coarse)
    beside = swaps(coarse, DEPTH)
    stats = pooled(exchanged(stats, ROWS), own)
    wide = jnp.concatenate([coarse] + beside, axis=1)
    beside = swaps(wide, ROWS)
    held = exchanged(stats, DEPTH)
    upper, lower, stats, _, _ = convolve(0, plane, block, whole, 1, at, held, norm_gain, norm_shift, [wide] + beside, conv_one)
    held = exchanged(pooled(exchanged(stats, ROWS), own), DEPTH)
    last, stats, gain, shift = convolve(1, plane, block, whole, 0, at, held, norm_gain, norm_shift, [upper, lower], conv_two)
    held = exchanged(pooled(exchanged(stats, ROWS), own), DEPTH)
    mean, spread = pooled(held, plane)
    scale = gain[0] / jnp.sqrt(spread / (plane * held.shape[0]) + 1e-05)
    features = leaky((last - mean) * scale + shift[0]).astype(jnp.bfloat16)
    return jnp.transpose(features, (3, 0, 1, 2))


def solution(mesh):
    split = Mesh(mesh.devices.reshape(4, 4, 2, 16), ROWS + (DEPTH,))
    return jax.shard_map(
        on_device,
        mesh=split,
        in_specs=(P(None, ROWS, DEPTH, None), P(), P(), P(), P(), P()),
        out_specs=P(None, ROWS, DEPTH, None),
        check_vma=False,
    )
```

```python
import functools

import jax
import jax.numpy as jnp
from jax import lax
from jax.experimental import pallas as pl
from jax.experimental.pallas import tpu as pltpu
from jax.sharding import Mesh
from jax.sharding import PartitionSpec as P


ROWS = ("x", "y", "core")
DEPTH = "z"


def swaps(value, axis):
    count = lax.axis_size(axis)
    even = [(i, i + 1) for i in range(0, count - 1, 2)]
    odd = [(i, i + 1) for i in range(1, count - 1, 2)]
    got = []
    for pairs in (even, odd):
        got.append(lax.ppermute(value, axis, pairs + [(j, i) for i, j in pairs]))
    return got


def exchanged(stats, axis):
    sent = jnp.broadcast_to(stats[None], (lax.axis_size(axis),) + stats.shape)
    return lax.all_to_all(sent, axis, 0, 0)


def pooled(held, count):
    mean = jnp.mean(held[:, 0], axis=0)
    apart = held[:, 0] - mean
    spread = jnp.sum(held[:, 1] + count * (apart * apart), axis=0)
    return jnp.stack([mean, spread])


def affine(held, count, gain, shift):
    parts = held.shape[0]
    means = [held[part, 0:1, :] for part in range(parts)]
    mean = sum(means) / parts
    spread = sum(
        held[part, 1:2, :] + count * ((means[part] - mean) * (means[part] - mean))
        for part in range(parts)
    )
    return mean, gain / jnp.sqrt(spread / (count * parts) + 1e-05), shift


def leaky(value):
    return jnp.where(value >= 0.0, value, 0.01 * value)


def orders(at, own, swapped):
    if not swapped:
        return [(0, 0, own)]
    odd = lax.rem(at, 2)
    return [(0, own, own), (own, (1 - odd) * 2 * own, own), (2 * own, odd * 2 * own, own)]


def conv_kernel(norm, count, block, whole, rim, swapped, at, held, gains, shifts, *refs):
    pieces, results = (3, 2) if swapped else (2, 1)
    fields, weight, outs, (stats, gain, moved, stacked, *fetching) = (
        refs[:pieces],
        refs[pieces],
        refs[pieces + 1 : pieces + 1 + results],
        refs[pieces + 1 + results :],
    )
    halves, fetches = [range(9)], [[]]
    if fetching:
        source, (weight, arrived, held_back) = weight, fetching
        halves = [range(0, 4), range(4, 9)]
        fetches = [
            [
                pltpu.make_async_copy(
                    source.at[tap // 3, tap % 3], weight.at[tap // 3, tap % 3], arrived.at[tap]
                )
                for tap in half
            ]
            for half in halves
        ]
        for fetch in fetches[0] + fetches[1]:
            fetch.start()
    length, channels = fields[0].shape[2:]
    rows, depth = pieces * fields[0].shape[0], 3 * block[1] if swapped else block[1] + 2

    mean, scale, shift = affine(held, count, gains[norm : norm + 1, :], shifts[norm : norm + 1, :])
    row_at = at[0] * block[0] - (rows - block[0]) // 2
    depth_at = at[1] * block[1] - (depth - block[1]) // 2
    each = fields[0].shape[0]
    row_groups = orders(at[0], block[0], True) if swapped else [(i * each, i * each, each) for i in range(pieces)]
    depth_groups = orders(at[1], block[1] if swapped else depth, swapped)
    for piece, (_, to_row, row_count) in enumerate(row_groups):
        for from_cell, to_cell, cell_count in depth_groups:
            for i in range(row_count):
                for j in range(cell_count):
                    row, cell = to_row + i, to_cell + j
                    y, z = row_at + row, depth_at + cell
                    here = (y >= 0) & (y < whole[0]) & (z >= 0) & (z < whole[1])
                    keep = jnp.where(here, 1.0, 0.0)
                    value = (fields[piece][i, from_cell + j] - mean) * (scale * keep) + shift * keep
                    value = jnp.maximum(value, 0.01 * value)
                    stacked[row * depth + cell] = value.astype(jnp.bfloat16)

    cells = depth - 2
    out = {row: outs[row * results // (rows - 2)].at[row % ((rows - 2) // results)] for row in range(rows - 2)}
    place = lax.broadcasted_iota(jnp.int32, (length, channels), 0)
    for number, half in enumerate(halves):
        for fetch in fetches[number]:
            fetch.wait()
        taps = jnp.concatenate(
            [
                jnp.concatenate(
                    [weight[tap // 3, tap % 3, :, part * channels : (part + 1) * channels] for tap in half],
                    axis=1,
                )
                for part in range(3)
            ],
            axis=0,
        )
        for row in range(rows - 2):
            taken = jnp.concatenate(
                [
                    stacked[pl.ds((row + tap // 3) * depth + tap % 3, cells)].reshape(cells * length, channels)
                    for tap in half
                ],
                axis=1,
            )
            product = lax.dot_general(
                taken, taps, (((1,), (1,)), ((), ())), preferred_element_type=jnp.float32
            )
            if number + 1 < len(halves):
                held_back[row] = product
                continue
            if number > 0:
                product = product + held_back[row]
            for cell in range(cells):
                before, here, after = (
                    product[cell * length : (cell + 1) * length, part * channels : (part + 1) * channels]
                    for part in range(3)
                )
                before = jnp.where(place > 0, pltpu.roll(before, 1, 0), 0.0)
                after = jnp.where(place < length - 1, pltpu.roll(after, length - 1, 0), 0.0)
                out[row][cell] = before + here + after

    inner = [
        out[row][cell]
        for row in range(rim, rows - 2 - rim)
        for cell in range(rim, cells - rim)
    ]
    middle = sum(jnp.sum(plane, axis=0, keepdims=True) for plane in inner) / (len(inner) * length)
    apart = [plane - middle for plane in inner]
    spread = sum(jnp.sum(plane * plane, axis=0, keepdims=True) for plane in apart)
    stats[0:1, :] = middle
    stats[1:2, :] = spread
    gain[...] = gains[norm + 1 : norm + 2, :]
    moved[...] = shifts[norm + 1 : norm + 2, :]


def convolve(norm, count, block, whole, rim, at, held, gains, shifts, fields, weight):
    pieces = len(fields)
    swapped = pieces == 3
    each, wide, length, channels = fields[0].shape
    rows, depth = pieces * each, wide if swapped else block[1] + 2
    in_vmem = pl.BlockSpec(memory_space=pltpu.VMEM)
    flops = 2 * (rows - 2) * (depth - 2) * length * channels * channels * 27
    row = jax.ShapeDtypeStruct((1, channels), jnp.float32)
    out = jax.ShapeDtypeStruct((rows - 2, depth - 2, length, channels), jnp.float32)
    outs = [jax.ShapeDtypeStruct(fields[0].shape, jnp.float32)] * 2 if swapped else [out]
    outs += [jax.ShapeDtypeStruct((2, channels), jnp.float32), row, row]
    scratch = [pltpu.VMEM((rows * depth, length, channels), jnp.bfloat16)]
    if swapped:
        scratch += [
            pltpu.VMEM(weight.shape, weight.dtype),
            pltpu.SemaphoreType.DMA((9,)),
            pltpu.VMEM((rows - 2, (depth - 2) * length, 3 * channels), jnp.float32),
        ]
        weight = pltpu.with_memory_space_constraint(weight, pltpu.HBM)
    return pl.pallas_call(
        functools.partial(conv_kernel, norm, count, block, whole, rim, swapped),
        out_shape=outs,
        in_specs=[pl.BlockSpec(memory_space=pltpu.SMEM)] + [in_vmem] * (3 + pieces)
        + [pl.BlockSpec(memory_space=pltpu.HBM) if swapped else in_vmem],
        out_specs=[in_vmem] * len(outs),
        scratch_shapes=scratch,
        input_output_aliases={5: 0, 6: 1} if swapped else {},
        compiler_params=pltpu.CompilerParams(vmem_limit_bytes=16 << 20),
        cost_estimate=pl.CostEstimate(flops=flops, bytes_accessed=2 << 20, transcendentals=0),
    )(at, held, gains, shifts, *fields, weight)


def strided(volume, down_weight):
    blocks = volume.reshape(
        volume.shape[0], volume.shape[1] // 2, 2, volume.shape[2] // 2, 2, volume.shape[3] // 2, 2
    )
    return jnp.einsum(
        "oiabc,iyazbxc->yzxo", down_weight, blocks, preferred_element_type=jnp.float32
    )


def local_moments(inner):
    mean = jnp.mean(inner, axis=(0, 1, 2))
    centered = inner - mean
    return jnp.stack([mean, jnp.sum(centered * centered, axis=(0, 1, 2))])


def on_device(volume, down_weight, conv_one, conv_two, norm_gain, norm_shift):
    coarse = strided(volume, down_weight)
    rows, depth, length = coarse.shape[:3]
    block = (rows, depth)
    whole = (rows * lax.axis_size(ROWS), depth * lax.axis_size(DEPTH))
    own = float(rows * depth * length)
    plane = own * lax.axis_size(ROWS)
    at = jnp.stack([lax.axis_index(ROWS), lax.axis_index(DEPTH)])
    coarse, at = lax.optimization_barrier((coarse, at))

    stats = local_moments(coarse)
    beside = swaps(coarse, DEPTH)
    stats = pooled(exchanged(stats, ROWS), own)
    wide = jnp.concatenate([coarse] + beside, axis=1)
    beside = swaps(wide, ROWS)
    held = exchanged(stats, DEPTH)
    upper, lower, stats, _, _ = convolve(0, plane, block, whole, 1, at, held, norm_gain, norm_shift, [wide] + beside, conv_one)
    held = exchanged(pooled(exchanged(stats, ROWS), own), DEPTH)
    last, stats, gain, shift = convolve(1, plane, block, whole, 0, at, held, norm_gain, norm_shift, [upper, lower], conv_two)
    held = exchanged(pooled(exchanged(stats, ROWS), own), DEPTH)
    mean, spread = pooled(held, plane)
    scale = gain[0] / jnp.sqrt(spread / (plane * held.shape[0]) + 1e-05)
    features = leaky((last - mean) * scale + shift[0]).astype(jnp.bfloat16)
    return jnp.transpose(features, (3, 0, 1, 2))


def solution(mesh):
    split = Mesh(mesh.devices.reshape(4, 4, 2, 16), ROWS + (DEPTH,))
    return jax.shard_map(
        on_device,
        mesh=split,
        in_specs=(P(None, ROWS, DEPTH, None), P(), P(), P(), P(), P()),
        out_specs=P(None, ROWS, DEPTH, None),
        check_vma=False,
    )
```
